1024 devices in a mesh: energy: 64 (over x, y, core), space: 16 (over z).
Axes of the slice: x: 4, y: 8, z: 16, core: 2. Of those that a mesh axis runs over, the one named last changes fastest.
Arguments:
- chain_map: float32 [2, 6144, 384], P(None, 'space'), may hold values from -0.21875 to 0.21875
- chain_source: float32 [2, 2048, 6144], P(None, 'energy', 'space'), may hold values from -4 to 4
- local_map: float32 [2, 6144, 768], P(None, 'space'), may hold values from -0.21875 to 0.21875
- local_source: float32 [2, 12288, 2048], P(None, 'space', 'energy'), may hold values from -6 to 6
- interaction: float32 [2, 16384, 2048], P(None, 'space', 'energy'), may hold values from -6 to 6
- element_pairs: int32 [2, 16384], P(None, 'space'), may hold values from 0 to 767, as said below
Outputs:
- self_energy: float32 [2, 16384, 2048], P(None, 'space', 'energy')
The draws below stay inside these ranges and needn't reach their ends.
Inputs may be any that keep to these rules, and one draw needn't show every extreme that they name: `element_pairs`: both orbitals of a selected element lie in the same block of 384 orbitals or in neighbouring blocks of its partition.
All inputs are finite; a program needn't handle non-finite values.
Results may differ from the reference program's by a relative error of at most 0.00011.
Values sent between devices are 32-bit elements; how exact they have to be, the bound alone decides.
No kernel may reach another device: no remote copies, remote signals or barrier semaphores. Data moves between devices by JAX's collectives and lax.ppermute only.
A program may use at most 64 MiB of HBM per device.

```python
import jax
import jax.numpy as jnp
from jax import lax

B = 384
LBLK = 2
NSEL_DEV = 1024
LOC = 768
NCHAIN = 6144
NORB = 12288
NE = 2048
NSEL_ALL = 16384
N_SPACE = 16


def draw_element_pairs(key, part):
    first_key, step_key, inner_key = jax.random.split(jax.random.fold_in(key, 17), 3)
    first_orbital = jax.random.randint(first_key, (NSEL_ALL,), 0, LOC)
    offsets = jax.random.randint(step_key, (NSEL_ALL,), -1, 2)
    second_block = jnp.clip(first_orbital // B + offsets, 0, LBLK - 1)
    second_orbital = second_block * B + jax.random.randint(inner_key, (NSEL_ALL,), 0, B)
    return jnp.stack([first_orbital, second_orbital]).astype(jnp.int32)


def levels(stream_key, extent, cuts, low, high):
    def one(axis_at, shards_of):
        steps = jax.random.uniform(jax.random.fold_in(jax.random.fold_in(stream_key, 6), axis_at), (shards_of,), jnp.float32, low / len(cuts), high / len(cuts))
        return jnp.repeat(jnp.exp(steps), extent[axis_at] // shards_of).reshape((-1,) + (1,) * (len(extent) - axis_at - 1))

    gain = one(*cuts[0])
    for cut in cuts[1:]:
        gain = gain * one(*cut)
    return gain


def centred(stream_key, shape, width, bound, shards=(), kind=jnp.bfloat16):
    values = width * jax.random.normal(stream_key, shape, jnp.float32)
    if shards:
        values = values * levels(stream_key, shape, shards, -0.22, 0.18)
    return jnp.clip(values, -bound, bound).astype(kind)


def setup_inputs(seed: int = 0) -> dict:
    arg_keys = jax.random.split(jax.random.key(seed), 7)
    return {
        "chain_map": centred(arg_keys[0], (2, NCHAIN, B), (2 * B) ** -0.5, 0.21875, ((1, 16),), jnp.float32),
        "chain_source": centred(arg_keys[1], (2, NE, NCHAIN), 0.25, 4.0, ((1, 64), (2, 16)), jnp.float32),
        "local_map": centred(arg_keys[2], (2, NCHAIN, LOC), (2 * B) ** -0.5, 0.21875, ((1, 16),), jnp.float32),
        "local_source": centred(arg_keys[3], (2, NORB, NE), 0.5, 6.0, ((1, 16), (2, 64)), jnp.float32),
        "interaction": centred(arg_keys[4], (2, NSEL_ALL, NE), 1.0, 6.0, ((1, 16), (2, 64)), jnp.float32),
        "element_pairs": draw_element_pairs(jax.random.fold_in(arg_keys[6], 71), 0),
    }


highest = lax.Precision.HIGHEST


def plain_dot(left_part, right_part):
    return jnp.dot(left_part, right_part, precision=highest, preferred_element_type=jnp.float32)


def across_dot(left_part, right_part):
    return lax.dot_general(left_part, right_part, (((0,), (1,)), ((), ())), precision=highest, preferred_element_type=jnp.float32)


def reference(chain_map, chain_source, local_map, local_source, interaction, element_pairs):
    state_re = jnp.zeros((NE, B), jnp.float32)
    state_im = jnp.zeros((NE, B), jnp.float32)
    pieces = []
    for partition in range(N_SPACE):
        chain_start = partition * B
        chain_stop = chain_start + B
        orbital_start = partition * LOC
        orbital_stop = orbital_start + LOC
        select_start = partition * NSEL_DEV
        select_stop = select_start + NSEL_DEV
        back_re = local_map[0, chain_start:chain_stop]
        back_im = local_map[1, chain_start:chain_stop]
        wave_re = across_dot(back_re, state_re) - across_dot(back_im, state_im) + local_source[0, orbital_start:orbital_stop]
        wave_im = across_dot(back_re, state_im) + across_dot(back_im, state_re) + local_source[1, orbital_start:orbital_stop]
        first_orbital = element_pairs[0, select_start:select_stop]
        second_orbital = element_pairs[1, select_start:select_stop]
        left_re = wave_re[first_orbital]
        left_im = wave_im[first_orbital]
        right_re = wave_re[second_orbital]
        right_im = wave_im[second_orbital]
        lesser_re = left_re * right_re + left_im * right_im
        lesser_im = left_im * right_re - left_re * right_im
        screened = interaction[0, select_start:select_stop] + 1j * interaction[1, select_start:select_stop]
        spectrum = jnp.fft.fft(lesser_re + 1j * lesser_im, axis=1) * jnp.fft.fft(screened, axis=1)
        response = jnp.fft.ifft(spectrum, axis=1) * (NE ** -0.5)
        pieces.append(jnp.stack([jnp.real(response), jnp.imag(response)]).astype(jnp.float32))
        coupling_re = chain_map[0, chain_start:chain_stop]
        coupling_im = chain_map[1, chain_start:chain_stop]
        new_re = plain_dot(state_re, coupling_re) - plain_dot(state_im, coupling_im) + chain_source[0, :, chain_start:chain_stop]
        new_im = plain_dot(state_re, coupling_im) + plain_dot(state_im, coupling_re) + chain_source[1, :, chain_start:chain_stop]
        state_re = new_re
        state_im = new_im
    return jnp.concatenate(pieces, axis=1)
```

```python
import jax
import jax.numpy as jnp
import numpy as np
from jax import lax
from jax.experimental import pallas as pl
from jax.experimental.pallas import tpu as pltpu
from jax.sharding import PartitionSpec as P

f32 = jnp.float32
bf16 = jnp.bfloat16


def call(kernel, out_shape, name, megabytes, scratch=()):
    return pl.pallas_call(
        kernel,
        out_shape=out_shape,
        scratch_shapes=list(scratch),
        name=name,
        compiler_params=pltpu.CompilerParams(vmem_limit_bytes=megabytes << 20),
    )


def halves(value):
    high = value.astype(bf16)
    return high, (value - high.astype(f32)).astype(bf16)


def dot(left, right):
    return jnp.dot(left, right, preferred_element_type=f32)


def complex_rows_dot(rows, high_ref, low_ref):
    count = rows.shape[0]
    high, low = halves(rows)
    both = dot(jnp.concatenate([high, low], axis=0), high_ref[...])
    product = both[:count] + both[count:] + dot(high, low_ref[...])
    half, width = count // 2, product.shape[1] // 2
    real = product[:half, :width] - product[half:, width:]
    imag = product[:half, width:] + product[half:, :width]
    return real, imag


def split_kernel(map_ref, high_ref, low_ref):
    width = map_ref.shape[2]
    for part in range(2):
        high, low = halves(map_ref[part])
        high_ref[:, part * width : (part + 1) * width] = high
        low_ref[:, part * width : (part + 1) * width] = low


def split_map(value):
    shape = jax.ShapeDtypeStruct((value.shape[1], 2 * value.shape[2]), bf16)
    return call(split_kernel, [shape, shape], "split_map", 8)(value)


def step_kernel(arrived_ref, state_ref, entering_ref, high_ref, low_ref, state_out, entering_out):
    arrived = arrived_ref[...]
    half = arrived.shape[0] // 2
    entering_out[...] = entering_ref[...] + arrived
    real, imag = complex_rows_dot(arrived, high_ref, low_ref)
    state_out[:half] = state_ref[:half] + real
    state_out[half:] = state_ref[half:] + imag


def chain_step(arrived, state, entering, high, low):
    shape = jax.ShapeDtypeStruct(state.shape, f32)
    return call(step_kernel, [shape, shape], "chain_step", 6)(arrived, state, entering, high, low)


def swap_blocks(parts):
    block = lax.broadcasted_iota(jnp.int32, parts[0].shape, 1) // 16
    for step in (1, 2, 4):
        clear = (block & step) == 0
        swapped = list(parts)
        for place in range(8):
            if place & step == 0:
                lower, upper = parts[place], parts[place + step]
                swapped[place] = jnp.where(clear, lower, pltpu.roll(upper, 16 * step, 1))
                swapped[place + step] = jnp.where(clear, pltpu.roll(lower, 128 - 16 * step, 1), upper)
        parts = swapped
    return parts


def pack(stage_ref, packed_ref):
    for group in range(8):
        parts = [stage_ref[b // 4, group, pl.ds(b % 4, 8, stride=4), :] for b in range(8)]
        for place, tile in enumerate(swap_blocks(parts)):
            packed_ref[8 * group + place] = tile


def pack_kernel(values_ref, packed_ref, stage_ref):
    for part in range(2):
        for group in range(8):
            stage_ref[part, group] = values_ref[part, :, group * 128 : (group + 1) * 128]
    pack(stage_ref, packed_ref)


def unpack_kernel(packed_ref, values_ref, stage_ref):
    for group in range(8):
        parts = [packed_ref[8 * group + place] for place in range(8)]
        for b, tile in enumerate(swap_blocks(parts)):
            stage_ref[b // 4, group, pl.ds(b % 4, 8, stride=4), :] = tile
    for part in range(2):
        for group in range(8):
            values_ref[part, :, group * 128 : (group + 1) * 128] = stage_ref[part, group]


def pack_array(values):
    shape = jax.ShapeDtypeStruct((64, 8, 128), f32)
    return call(pack_kernel, shape, "pack_screened", 4, [pltpu.VMEM((2, 8, 32, 128), f32)])(values)


def unpack_array(packed):
    shape = jax.ShapeDtypeStruct((2, 32, 1024), f32)
    return call(unpack_kernel, shape, "unpack_result", 4, [pltpu.VMEM((2, 8, 32, 128), f32)])(packed)


def choose_kernel(pairs_ref, chosen_ref):
    orbitals, count = chosen_ref.shape[0], pairs_ref.shape[1]
    for side in range(2):
        for group in range(count // 128):
            wanted = pairs_ref[side : side + 1, group * 128 : (group + 1) * 128]
            rows = lax.broadcasted_iota(jnp.int32, (orbitals, 128), 0)
            column = side * count + group * 128
            chosen_ref[:, column : column + 128] = jnp.where(rows == wanted, 1.0, 0.0).astype(bf16)


def choose(pairs, orbitals):
    shape = jax.ShapeDtypeStruct((orbitals, 2 * pairs.shape[1]), bf16)
    return call(choose_kernel, shape, "choose", 8)(pairs)


def lesser_kernel(
    arrived_ref, entering_ref, high_ref, low_ref, source_ref, chosen_ref, packed_ref, stage_ref
):
    state = entering_ref[...] + arrived_ref[...]
    real, imag = complex_rows_dot(state, high_ref, low_ref)
    wave = jnp.concatenate([real + source_ref[0], imag + source_ref[1]], axis=0)
    rows, half = wave.shape[0], wave.shape[0] // 2
    high, low = halves(wave)
    both = dot(jnp.concatenate([high, low], axis=0), chosen_ref[...])
    taken = both[:rows] + both[rows:]
    count = taken.shape[1] // 2
    left_re, left_im = taken[:half, :count], taken[half:, :count]
    right_re, right_im = taken[:half, count:], taken[half:, count:]
    lesser_re = left_re * right_re + left_im * right_im
    lesser_im = left_im * right_re - left_re * right_im
    for group in range(8):
        stage_ref[0, group] = lesser_re[:, group * 128 : (group + 1) * 128]
        stage_ref[1, group] = lesser_im[:, group * 128 : (group + 1) * 128]
    pack(stage_ref, packed_ref)


def packed_lesser(arrived, entering, high, low, source, chosen):
    shape = jax.ShapeDtypeStruct((64, 8, 128), f32)
    scratch = [pltpu.VMEM((2, 8, 32, 128), f32)]
    return call(lesser_kernel, shape, "packed_lesser", 14, scratch)(
        arrived, entering, high, low, source, chosen
    )


def small_tables():
    coarse, fine = 32 * np.arange(16)[:, None], np.arange(32)[:, None]
    column, lane = np.arange(512)[None, :], np.arange(128)
    imaginary, phase, element = lane // 64, lane // 16 % 4, lane % 16

    def both(rows, columns, period):
        angle = 2.0 * np.pi / period * (rows * columns % period)
        return np.stack([np.cos(angle), np.sin(angle)]).astype(np.float32)

    turns = phase[:, None] * phase[None, :] % 4
    cosine, sine = np.array([1, 0, -1, 0])[turns], np.array([0, 1, 0, -1])[turns]
    sign = imaginary[:, None] - imaginary[None, :]
    same = element[:, None] == element[None, :]
    forward = np.where(sign == 0, cosine, sign * sine) * same
    backward = np.where(sign == 0, cosine, -sign * sine) * same
    lanes = np.stack([forward, backward]).astype(jnp.bfloat16)
    return (
        both(coarse, column, 512),
        both(fine, column, 512),
        both(coarse, phase[None, :], 2048),
        both(fine, phase[None, :], 2048),
        lanes,
    )


def tables_kernel(coarse_ref, fine_ref, outer_ref, inner_ref, high_ref, low_ref, twiddle_ref):
    lane = lax.broadcasted_iota(jnp.int32, (32, 128), 1)
    for place in range(16):
        rows = slice(32 * place, 32 * place + 32)
        cosine, sine = coarse_ref[0, place : place + 1], coarse_ref[1, place : place + 1]
        high, low = halves(cosine * fine_ref[0] - sine * fine_ref[1])
        high_ref[rows, :512], low_ref[rows, :512] = high, low
        high, low = halves(sine * fine_ref[0] + cosine * fine_ref[1])
        high_ref[rows, 512:], low_ref[rows, 512:] = high, low
        cosine, sine = outer_ref[0, place : place + 1], outer_ref[1, place : place + 1]
        twiddle_ref[0, rows] = cosine * inner_ref[0] - sine * inner_ref[1]
        turn = sine * inner_ref[0] + cosine * inner_ref[1]
        twiddle_ref[1, rows] = jnp.where(lane < 64, turn, -turn)


def tables():
    *small, lanes = small_tables()
    waves = jax.ShapeDtypeStruct((512, 1024), bf16)
    shapes = [waves, waves, jax.ShapeDtypeStruct((2, 512, 128), f32)]
    return (*call(tables_kernel, shapes, "tables", 8)(*small), lanes)


def turned(value):
    lane = lax.broadcasted_iota(jnp.int32, value.shape, 1)
    rolled = pltpu.roll(value, 64, 1)
    return jnp.where(lane < 64, rolled, -rolled)


def rows_transform(value, other, high_ref, low_ref):
    high, low = halves(jnp.concatenate([value, other], axis=0))
    both = dot(high_ref[...], jnp.concatenate([high, low], axis=1))
    return both[:, :128] + both[:, 128:] + dot(low_ref[...], high)


def lanes_transform(value, table):
    high, low = halves(value)
    return dot(high, table) + dot(low, table)


def spectrum_of(packed_ref, high_ref, low_ref, twiddle_ref, lanes_ref):
    value = packed_ref[...].reshape(512, 128)
    value = rows_transform(value, turned(value), high_ref, low_ref)
    value = value * twiddle_ref[0] + pltpu.roll(value, 64, 1) * twiddle_ref[1]
    return lanes_transform(value, lanes_ref[0])


def screened_kernel(packed_ref, high_ref, low_ref, twiddle_ref, lanes_ref, out_ref):
    value = spectrum_of(packed_ref, high_ref, low_ref, twiddle_ref, lanes_ref) * (2048.0**-1.5)
    rolled = pltpu.roll(value, 64, 1)
    first = lax.broadcasted_iota(jnp.int32, value.shape, 1) < 64
    out_ref[0] = jnp.where(first, value, rolled)
    out_ref[1] = jnp.where(first, -rolled, value)


def convolve_kernel(packed_ref, screened_ref, high_ref, low_ref, twiddle_ref, lanes_ref, out_ref):
    value = spectrum_of(packed_ref, high_ref, low_ref, twiddle_ref, lanes_ref)
    value = value * screened_ref[0] + pltpu.roll(value, 64, 1) * screened_ref[1]
    value = lanes_transform(value, lanes_ref[1])
    value = value * twiddle_ref[0] - pltpu.roll(value, 64, 1) * twiddle_ref[1]
    value = rows_transform(value, -turned(value), high_ref, low_ref)
    out_ref[...] = value.reshape(64, 8, 128)


def screened_spectrum(packed, constants):
    shape = jax.ShapeDtypeStruct((2, 512, 128), f32)
    return call(screened_kernel, shape, "screened_spectrum", 8)(packed, *constants)


def convolve(packed, screened, constants):
    shape = jax.ShapeDtypeStruct((64, 8, 128), f32)
    return call(convolve_kernel, shape, "convolve", 8)(packed, screened, *constants)


def exchange(packed):
    return lax.all_to_all(packed, "energy", split_axis=0, concat_axis=0, tiled=True)


def body(chain_map, chain_source, local_map, local_source, interaction, element_pairs):
    constants = tables()
    partitions = lax.axis_size("space")
    rows = 2 * chain_source.shape[1]
    state = chain_source.reshape(rows, chain_source.shape[2])
    entering = jnp.zeros_like(state)
    map_high, map_low = split_map(chain_map)
    for place in range(1, partitions):
        arrived = lax.ppermute(state, "space", [(place - 1, place)])
        if place < partitions - 1:
            state, entering = chain_step(arrived, state, entering, map_high, map_low)
    screened = exchange(pack_array(jnp.swapaxes(interaction, 1, 2)))
    screened = screened_spectrum(screened, constants)
    local_high, local_low = split_map(local_map)
    chosen = choose(element_pairs, local_map.shape[2])
    source = jnp.swapaxes(local_source, 1, 2)
    packed = packed_lesser(arrived, entering, local_high, local_low, source, chosen)
    result = convolve(exchange(packed), screened, constants)
    return jnp.swapaxes(unpack_array(exchange(result)), 1, 2)


def solution(mesh):
    in_specs = (
        P(None, "space", None),
        P(None, "energy", "space"),
        P(None, "space", None),
        P(None, "space", "energy"),
        P(None, "space", "energy"),
        P(None, "space"),
    )
    out_specs = P(None, "space", "energy")
    return jax.shard_map(body, mesh=mesh, in_specs=in_specs, out_specs=out_specs, check_vma=False)
```

```python
import functools

import jax
import jax.numpy as jnp
import numpy as np
from jax import lax
from jax.experimental import pallas as pl
from jax.experimental.pallas import tpu as pltpu
from jax.sharding import PartitionSpec as P


SINGLES = 5
LEADERS = (7, 10, 13)

f32 = jnp.float32
bf16 = jnp.bfloat16


def call(kernel, out_shape, megabytes, scratch=()):
    return pl.pallas_call(
        kernel,
        out_shape=out_shape,
        scratch_shapes=list(scratch),
        compiler_params=pltpu.CompilerParams(vmem_limit_bytes=megabytes << 20),
    )


def halves(value):
    high = value.astype(bf16)
    return high, (value - high.astype(f32)).astype(bf16)


def dot(left, right):
    return jnp.dot(left, right, preferred_element_type=f32)


def complex_rows_dot(rows, high_ref, low_ref):
    count = rows.shape[0]
    high, low = halves(rows)
    both = dot(jnp.concatenate([high, low], axis=0), high_ref[...])
    product = both[:count] + both[count:] + dot(high, low_ref[...])
    half, width = count // 2, product.shape[1] // 2
    real = product[:half, :width] - product[half:, width:]
    imag = product[:half, width:] + product[half:, :width]
    return real, imag


def split_kernel(map_ref, high_ref, low_ref):
    width = map_ref.shape[2]
    for part in range(2):
        high, low = halves(map_ref[part])
        high_ref[:, part * width : (part + 1) * width] = high
        low_ref[:, part * width : (part + 1) * width] = low


def split_map(value):
    shape = jax.ShapeDtypeStruct((value.shape[1], 2 * value.shape[2]), bf16)
    return call(split_kernel, [shape, shape], 8)(value)


def advanced(state, high_ref, low_ref, source_ref):
    real, imag = complex_rows_dot(state, high_ref, low_ref)
    return jnp.concatenate([real, imag], axis=0) + source_ref[...]


def first_kernel(number, place_ref, arrived_ref, *refs):
    operands, (entering_ref, middle_ref, state_ref) = refs[:3], refs[3:]
    middle_ref[...] = jnp.zeros_like(middle_ref)

    @pl.when(place_ref[0] == number)
    def _():
        arrived = arrived_ref[...]
        entering_ref[...] = arrived
        state_ref[...] = advanced(arrived, *operands)

    @pl.when(place_ref[0] != number)
    def _():
        entering_ref[...] = jnp.zeros_like(entering_ref)
        state_ref[...] = jnp.zeros_like(state_ref)


def single_kernel(number, place_ref, arrived_ref, *refs):
    operands, (entering_ref, state_ref) = refs[:3], refs[5:]

    @pl.when(place_ref[0] == number)
    def _():
        arrived = arrived_ref[...]
        entering_ref[...] = arrived
        state_ref[...] = advanced(arrived, *operands)


def triple_kernel(number, place_ref, arrived_ref, *refs):
    before, own, after = refs[0:3], refs[3:6], refs[6:9]
    entering_ref, middle_ref, state_ref = refs[12:]

    @pl.when(place_ref[0] == number)
    def _():
        first = advanced(arrived_ref[...], *before)
        entering_ref[...] = first
        second = advanced(first, *own)
        middle_ref[...] = second
        state_ref[...] = advanced(second, *after)


def on_plane(kernel, number, place, operands, held, fresh=()):
    vmem = pl.BlockSpec(memory_space=pltpu.VMEM)
    count = 1 + len(operands)
    results = (*held, *fresh)
    return pl.pallas_call(
        functools.partial(kernel, number),
        out_shape=[jax.ShapeDtypeStruct(value.shape, value.dtype) for value in results],
        in_specs=[pl.BlockSpec(memory_space=pltpu.SMEM)] + [vmem] * (len(operands) + len(held)),
        out_specs=[vmem] * len(results),
        input_output_aliases={count + index: index for index in range(len(held))},
        compiler_params=pltpu.CompilerParams(vmem_limit_bytes=6 << 20),
    )(place, *operands, *held)


def swap_blocks(parts):
    block = lax.broadcasted_iota(jnp.int32, parts[0].shape, 1) // 16
    for step in (1, 2, 4):
        clear = (block & step) == 0
        swapped = list(parts)
        for place in range(8):
            if place & step == 0:
                lower, upper = parts[place], parts[place + step]
                swapped[place] = jnp.where(clear, lower, pltpu.roll(upper, 16 * step, 1))
                swapped[place + step] = jnp.where(clear, pltpu.roll(lower, 128 - 16 * step, 1), upper)
        parts = swapped
    return parts


def pack(stage_ref, packed_ref):
    for group in range(8):
        parts = [stage_ref[b // 4, group, pl.ds(b % 4, 8, stride=4), :] for b in range(8)]
        for place, tile in enumerate(swap_blocks(parts)):
            packed_ref[8 * group + place] = tile


def pack_kernel(values_ref, packed_ref, stage_ref):
    for part in range(2):
        for group in range(8):
            stage_ref[part, group] = values_ref[part, :, group * 128 : (group + 1) * 128]
    pack(stage_ref, packed_ref)


def unpack_kernel(packed_ref, values_ref, stage_ref):
    for group in range(8):
        parts = [packed_ref[8 * group + place] for place in range(8)]
        for b, tile in enumerate(swap_blocks(parts)):
            stage_ref[b // 4, group, pl.ds(b % 4, 8, stride=4), :] = tile
    for part in range(2):
        for group in range(8):
            values_ref[part, :, group * 128 : (group + 1) * 128] = stage_ref[part, group]


def pack_array(values):
    shape = jax.ShapeDtypeStruct((64, 8, 128), f32)
    return call(pack_kernel, shape, 4, [pltpu.VMEM((2, 8, 32, 128), f32)])(values)


def unpack_array(packed):
    shape = jax.ShapeDtypeStruct((2, 32, 1024), f32)
    return call(unpack_kernel, shape, 4, [pltpu.VMEM((2, 8, 32, 128), f32)])(packed)


def choose_kernel(pairs_ref, chosen_ref):
    orbitals, count = chosen_ref.shape[0], pairs_ref.shape[1]
    for side in range(2):
        for group in range(count // 128):
            wanted = pairs_ref[side : side + 1, group * 128 : (group + 1) * 128]
            rows = lax.broadcasted_iota(jnp.int32, (orbitals, 128), 0)
            column = side * count + group * 128
            chosen_ref[:, column : column + 128] = jnp.where(rows == wanted, 1.0, 0.0).astype(bf16)


def choose(pairs, orbitals):
    shape = jax.ShapeDtypeStruct((orbitals, 2 * pairs.shape[1]), bf16)
    return call(choose_kernel, shape, 8)(pairs)


def lesser_kernel(
    arrived_ref, other_ref, entering_ref, high_ref, low_ref, source_ref, chosen_ref, packed_ref, stage_ref
):
    state = entering_ref[...] + (arrived_ref[...] + other_ref[...])
    real, imag = complex_rows_dot(state, high_ref, low_ref)
    wave = jnp.concatenate([real + source_ref[0], imag + source_ref[1]], axis=0)
    rows, half = wave.shape[0], wave.shape[0] // 2
    high, low = halves(wave)
    both = dot(jnp.concatenate([high, low], axis=0), chosen_ref[...])
    taken = both[:rows] + both[rows:]
    count = taken.shape[1] // 2
    left_re, left_im = taken[:half, :count], taken[half:, :count]
    right_re, right_im = taken[:half, count:], taken[half:, count:]
    lesser_re = left_re * right_re + left_im * right_im
    lesser_im = left_im * right_re - left_re * right_im
    for group in range(8):
        stage_ref[0, group] = lesser_re[:, group * 128 : (group + 1) * 128]
        stage_ref[1, group] = lesser_im[:, group * 128 : (group + 1) * 128]
    pack(stage_ref, packed_ref)


def packed_lesser(arrived, other, entering, high, low, source, chosen):
    shape = jax.ShapeDtypeStruct((64, 8, 128), f32)
    scratch = [pltpu.VMEM((2, 8, 32, 128), f32)]
    return call(lesser_kernel, shape, 14, scratch)(
        arrived, other, entering, high, low, source, chosen
    )


def small_tables():
    coarse, fine = 32 * np.arange(16)[:, None], np.arange(32)[:, None]
    column, lane = np.arange(512)[None, :], np.arange(128)
    imaginary, phase, element = lane // 64, lane // 16 % 4, lane % 16

    def both(rows, columns, period):
        angle = 2.0 * np.pi / period * (rows * columns % period)
        return np.stack([np.cos(angle), np.sin(angle)]).astype(np.float32)

    turns = phase[:, None] * phase[None, :] % 4
    cosine, sine = np.array([1, 0, -1, 0])[turns], np.array([0, 1, 0, -1])[turns]
    sign = imaginary[:, None] - imaginary[None, :]
    same = element[:, None] == element[None, :]
    forward = np.where(sign == 0, cosine, sign * sine) * same
    backward = np.where(sign == 0, cosine, -sign * sine) * same
    lanes = np.stack([forward, backward]).astype(jnp.bfloat16)
    return (
        both(coarse, column, 512),
        both(fine, column, 512),
        both(coarse, phase[None, :], 2048),
        both(fine, phase[None, :], 2048),
        lanes,
    )


def tables_kernel(coarse_ref, fine_ref, outer_ref, inner_ref, high_ref, low_ref, twiddle_ref):
    lane = lax.broadcasted_iota(jnp.int32, (32, 128), 1)
    for place in range(16):
        rows = slice(32 * place, 32 * place + 32)
        cosine, sine = coarse_ref[0, place : place + 1], coarse_ref[1, place : place + 1]
        high, low = halves(cosine * fine_ref[0] - sine * fine_ref[1])
        high_ref[rows, :512], low_ref[rows, :512] = high, low
        high, low = halves(sine * fine_ref[0] + cosine * fine_ref[1])
        high_ref[rows, 512:], low_ref[rows, 512:] = high, low
        cosine, sine = outer_ref[0, place : place + 1], outer_ref[1, place : place + 1]
        twiddle_ref[0, rows] = cosine * inner_ref[0] - sine * inner_ref[1]
        turn = sine * inner_ref[0] + cosine * inner_ref[1]
        twiddle_ref[1, rows] = jnp.where(lane < 64, turn, -turn)


def tables():
    *small, lanes = small_tables()
    waves = jax.ShapeDtypeStruct((512, 1024), bf16)
    shapes = [waves, waves, jax.ShapeDtypeStruct((2, 512, 128), f32)]
    return (*call(tables_kernel, shapes, 8)(*small), lanes)


def turned(value):
    lane = lax.broadcasted_iota(jnp.int32, value.shape, 1)
    rolled = pltpu.roll(value, 64, 1)
    return jnp.where(lane < 64, rolled, -rolled)


def rows_transform(value, other, high_ref, low_ref):
    high, low = halves(jnp.concatenate([value, other], axis=0))
    both = dot(high_ref[...], jnp.concatenate([high, low], axis=1))
    return both[:, :128] + both[:, 128:] + dot(low_ref[...], high)


def lanes_transform(value, table):
    high, low = halves(value)
    return dot(high, table) + dot(low, table)


def spectrum_of(packed_ref, high_ref, low_ref, twiddle_ref, lanes_ref):
    value = packed_ref[...].reshape(512, 128)
    value = rows_transform(value, turned(value), high_ref, low_ref)
    value = value * twiddle_ref[0] + pltpu.roll(value, 64, 1) * twiddle_ref[1]
    return lanes_transform(value, lanes_ref[0])


def screened_kernel(packed_ref, high_ref, low_ref, twiddle_ref, lanes_ref, out_ref):
    value = spectrum_of(packed_ref, high_ref, low_ref, twiddle_ref, lanes_ref) * (2048.0**-1.5)
    rolled = pltpu.roll(value, 64, 1)
    first = lax.broadcasted_iota(jnp.int32, value.shape, 1) < 64
    out_ref[0] = jnp.where(first, value, rolled)
    out_ref[1] = jnp.where(first, -rolled, value)


def convolve_kernel(packed_ref, screened_ref, high_ref, low_ref, twiddle_ref, lanes_ref, out_ref):
    value = spectrum_of(packed_ref, high_ref, low_ref, twiddle_ref, lanes_ref)
    value = value * screened_ref[0] + pltpu.roll(value, 64, 1) * screened_ref[1]
    value = lanes_transform(value, lanes_ref[1])
    value = value * twiddle_ref[0] - pltpu.roll(value, 64, 1) * twiddle_ref[1]
    value = rows_transform(value, -turned(value), high_ref, low_ref)
    out_ref[...] = value.reshape(64, 8, 128)


def screened_spectrum(packed, constants):
    shape = jax.ShapeDtypeStruct((2, 512, 128), f32)
    return call(screened_kernel, shape, 8)(packed, *constants)


def convolve(packed, screened, constants):
    shape = jax.ShapeDtypeStruct((64, 8, 128), f32)
    return call(convolve_kernel, shape, 8)(packed, screened, *constants)


def exchange(packed):
    return lax.all_to_all(packed, "energy", split_axis=0, concat_axis=0, tiled=True)


def body(chain_map, chain_source, local_map, local_source, interaction, element_pairs):
    constants = tables()
    place = lax.axis_index("space").astype(jnp.int32).reshape(1)
    rows = 2 * chain_source.shape[1]
    source = chain_source.reshape(rows, chain_source.shape[2])

    def move(value, *pairs):
        return lax.ppermute(value, "space", pairs)

    arrived = move(source, (0, 1))
    upward = [(leader - 1, leader) for leader in LEADERS]
    downward = [(leader + 1, leader) for leader in LEADERS]
    before = (move(chain_map, *upward), move(source, *upward))
    after = (move(chain_map, *downward), move(source, *downward))
    own = (*split_map(chain_map), source)
    entering, middle, state = on_plane(first_kernel, 1, place, (arrived, *own), (), (source,) * 3)
    for number in range(2, SINGLES + 1):
        arrived = move(state, (number - 1, number))
        entering, state = on_plane(
            single_kernel, number, place, (arrived, *own), (entering, state)
        )
    before = (*split_map(before[0]), before[1])
    after = (*split_map(after[0]), after[1])
    last = SINGLES
    for leader in LEADERS:
        arrived = move(state, (last, leader))
        operands = (arrived, *before, *own, *after)
        entering, middle, state = on_plane(
            triple_kernel, leader, place, operands, (entering, middle, state)
        )
        last = leader
    arrived = move(state, (SINGLES, SINGLES + 1), *((leader, leader + 2) for leader in LEADERS))
    other = move(middle, *((leader, leader + 1) for leader in LEADERS))
    screened = exchange(pack_array(jnp.swapaxes(interaction, 1, 2)))
    screened = screened_spectrum(screened, constants)
    local_high, local_low = split_map(local_map)
    chosen = choose(element_pairs, local_map.shape[2])
    constant = jnp.swapaxes(local_source, 1, 2)
    packed = packed_lesser(arrived, other, entering, local_high, local_low, constant, chosen)
    result = convolve(exchange(packed), screened, constants)
    return jnp.swapaxes(unpack_array(exchange(result)), 1, 2)


def solution(mesh):
    in_specs = (
        P(None, "space", None),
        P(None, "energy", "space"),
        P(None, "space", None),
        P(None, "space", "energy"),
        P(None, "space", "energy"),
        P(None, "space"),
    )
    out_specs = P(None, "space", "energy")

    return jax.shard_map(body, mesh=mesh, in_specs=in_specs, out_specs=out_specs, check_vma=False)
```

```python
import functools

import jax
import jax.numpy as jnp
import numpy as np
from jax import lax
from jax.experimental import pallas as pl
from jax.experimental.pallas import tpu as pltpu
from jax.sharding import PartitionSpec as P


SINGLES = 5
LEADERS = (7, 10, 13)

f32 = jnp.float32
bf16 = jnp.bfloat16


def call(kernel, out_shape, megabytes, scratch=(), awaits=False):
    if awaits:
        vmem = pl.BlockSpec(memory_space=pltpu.VMEM)

        def after(*operands):
            specs = [vmem] * (len(operands) - 1) + [pl.BlockSpec(memory_space=pl.ANY)]
            count = len(operands) - 1

            def body(*refs):
                kernel(*refs[:count], *refs[count + 1 :])

            return pl.pallas_call(
                body,
                out_shape=out_shape,
                in_specs=specs,
                compiler_params=pltpu.CompilerParams(vmem_limit_bytes=megabytes << 20),
            )(*operands)

        return after
    return pl.pallas_call(
        kernel,
        out_shape=out_shape,
        scratch_shapes=list(scratch),
        compiler_params=pltpu.CompilerParams(vmem_limit_bytes=megabytes << 20),
    )


def halves(value):
    high = value.astype(bf16)
    return high, (value - high.astype(f32)).astype(bf16)


def dot(left, right):
    return jnp.dot(left, right, preferred_element_type=f32)


def complex_rows_dot(rows, high_ref, low_ref):
    count = rows.shape[0]
    high, low = halves(rows)
    both = dot(jnp.concatenate([high, low], axis=0), high_ref[...])
    product = both[:count] + both[count:] + dot(high, low_ref[...])
    half, width = count // 2, product.shape[1] // 2
    real = product[:half, :width] - product[half:, width:]
    imag = product[:half, width:] + product[half:, :width]
    return real, imag


def split_kernel(map_ref, high_ref, low_ref):
    width = map_ref.shape[2]
    for part in range(2):
        high, low = halves(map_ref[part])
        high_ref[:, part * width : (part + 1) * width] = high
        low_ref[:, part * width : (part + 1) * width] = low


def split_map(value, *awaited):
    shape = jax.ShapeDtypeStruct((value.shape[1], 2 * value.shape[2]), bf16)
    return call(split_kernel, [shape, shape], 8, (), bool(awaited))(value, *awaited)


def advanced(state, high_ref, low_ref, source_ref):
    real, imag = complex_rows_dot(state, high_ref, low_ref)
    return jnp.concatenate([real, imag], axis=0) + source_ref[...]


def first_kernel(number, place_ref, arrived_ref, *refs):
    operands, (entering_ref, middle_ref, state_ref) = refs[:3], refs[3:]
    middle_ref[...] = jnp.zeros_like(middle_ref)

    @pl.when(place_ref[0] == number)
    def _():
        arrived = arrived_ref[...]
        entering_ref[...] = arrived
        state_ref[...] = advanced(arrived, *operands)

    @pl.when(place_ref[0] != number)
    def _():
        entering_ref[...] = jnp.zeros_like(entering_ref)
        state_ref[...] = jnp.zeros_like(state_ref)


def single_kernel(number, place_ref, arrived_ref, *refs):
    operands, held, (entering_ref, state_ref) = refs[:3], refs[3:5], refs[5:]

    @pl.when(place_ref[0] == number)
    def _():
        arrived = arrived_ref[...]
        entering_ref[...] = arrived
        state_ref[...] = advanced(arrived, *operands)

    @pl.when(place_ref[0] != number)
    def _():
        for before_ref, after_ref in zip(held, (entering_ref, state_ref)):
            after_ref[...] = before_ref[...]


def triple_kernel(number, place_ref, arrived_ref, *refs):
    before, own, after = refs[0:3], refs[3:6], refs[6:9]
    held, (entering_ref, middle_ref, state_ref) = refs[9:12], refs[12:]

    @pl.when(place_ref[0] == number)
    def _():
        first = advanced(arrived_ref[...], *before)
        entering_ref[...] = first
        second = advanced(first, *own)
        middle_ref[...] = second
        state_ref[...] = advanced(second, *after)

    @pl.when(place_ref[0] != number)
    def _():
        for before_ref, after_ref in zip(held, (entering_ref, middle_ref, state_ref)):
            after_ref[...] = before_ref[...]


def on_plane(kernel, number, place, operands, held, fresh=()):
    vmem = pl.BlockSpec(memory_space=pltpu.VMEM)
    results = (*held, *fresh)
    return pl.pallas_call(
        functools.partial(kernel, number),
        out_shape=[jax.ShapeDtypeStruct(value.shape, value.dtype) for value in results],
        in_specs=[pl.BlockSpec(memory_space=pltpu.SMEM)] + [vmem] * (len(operands) + len(held)),
        out_specs=[vmem] * len(results),
        compiler_params=pltpu.CompilerParams(vmem_limit_bytes=6 << 20),
    )(place, *operands, *held)


def swap_blocks(parts):
    block = lax.broadcasted_iota(jnp.int32, parts[0].shape, 1) // 16
    for step in (1, 2, 4):
        clear = (block & step) == 0
        swapped = list(parts)
        for place in range(8):
            if place & step == 0:
                lower, upper = parts[place], parts[place + step]
                swapped[place] = jnp.where(clear, lower, pltpu.roll(upper, 16 * step, 1))
                swapped[place + step] = jnp.where(clear, pltpu.roll(lower, 128 - 16 * step, 1), upper)
        parts = swapped
    return parts


def pack(stage_ref, packed_ref):
    for group in range(8):
        parts = [stage_ref[b // 4, group, pl.ds(b % 4, 8, stride=4), :] for b in range(8)]
        for place, tile in enumerate(swap_blocks(parts)):
            packed_ref[8 * group + place] = tile


def pack_kernel(values_ref, packed_ref, stage_ref):
    for part in range(2):
        for group in range(8):
            stage_ref[part, group] = values_ref[part, :, group * 128 : (group + 1) * 128]
    pack(stage_ref, packed_ref)


def unpack_kernel(packed_ref, values_ref, stage_ref):
    for group in range(8):
        parts = [packed_ref[8 * group + place] for place in range(8)]
        for b, tile in enumerate(swap_blocks(parts)):
            stage_ref[b // 4, group, pl.ds(b % 4, 8, stride=4), :] = tile
    for part in range(2):
        for group in range(8):
            values_ref[part, :, group * 128 : (group + 1) * 128] = stage_ref[part, group]


def pack_array(values):
    shape = jax.ShapeDtypeStruct((64, 8, 128), f32)
    return call(pack_kernel, shape, 4, [pltpu.VMEM((2, 8, 32, 128), f32)])(values)


def unpack_array(packed):
    shape = jax.ShapeDtypeStruct((2, 32, 1024), f32)
    return call(unpack_kernel, shape, 4, [pltpu.VMEM((2, 8, 32, 128), f32)])(packed)


def choose_kernel(pairs_ref, chosen_ref):
    orbitals, count = chosen_ref.shape[0], pairs_ref.shape[1]
    for side in range(2):
        for group in range(count // 128):
            wanted = pairs_ref[side : side + 1, group * 128 : (group + 1) * 128]
            rows = lax.broadcasted_iota(jnp.int32, (orbitals, 128), 0)
            column = side * count + group * 128
            chosen_ref[:, column : column + 128] = jnp.where(rows == wanted, 1.0, 0.0).astype(bf16)


def choose(pairs, orbitals):
    shape = jax.ShapeDtypeStruct((orbitals, 2 * pairs.shape[1]), bf16)
    return call(choose_kernel, shape, 8)(pairs)


def lesser_kernel(
    arrived_ref, other_ref, entering_ref, high_ref, low_ref, source_ref, chosen_ref, packed_ref, stage_ref
):
    state = entering_ref[...] + (arrived_ref[...] + other_ref[...])
    real, imag = complex_rows_dot(state, high_ref, low_ref)
    wave = jnp.concatenate([real + source_ref[0], imag + source_ref[1]], axis=0)
    rows, half = wave.shape[0], wave.shape[0] // 2
    high, low = halves(wave)
    both = dot(jnp.concatenate([high, low], axis=0), chosen_ref[...])
    taken = both[:rows] + both[rows:]
    count = taken.shape[1] // 2
    left_re, left_im = taken[:half, :count], taken[half:, :count]
    right_re, right_im = taken[:half, count:], taken[half:, count:]
    lesser_re = left_re * right_re + left_im * right_im
    lesser_im = left_im * right_re - left_re * right_im
    for group in range(8):
        stage_ref[0, group] = lesser_re[:, group * 128 : (group + 1) * 128]
        stage_ref[1, group] = lesser_im[:, group * 128 : (group + 1) * 128]
    pack(stage_ref, packed_ref)


def packed_lesser(arrived, other, entering, high, low, source, chosen):
    shape = jax.ShapeDtypeStruct((64, 8, 128), f32)
    scratch = [pltpu.VMEM((2, 8, 32, 128), f32)]
    return call(lesser_kernel, shape, 14, scratch)(
        arrived, other, entering, high, low, source, chosen
    )


def small_tables():
    coarse, fine = 32 * np.arange(16)[:, None], np.arange(32)[:, None]
    column, lane = np.arange(512)[None, :], np.arange(128)
    imaginary, phase, element = lane // 64, lane // 16 % 4, lane % 16

    def both(rows, columns, period):
        angle = 2.0 * np.pi / period * (rows * columns % period)
        return np.stack([np.cos(angle), np.sin(angle)]).astype(np.float32)

    turns = phase[:, None] * phase[None, :] % 4
    cosine, sine = np.array([1, 0, -1, 0])[turns], np.array([0, 1, 0, -1])[turns]
    sign = imaginary[:, None] - imaginary[None, :]
    same = element[:, None] == element[None, :]
    forward = np.where(sign == 0, cosine, sign * sine) * same
    backward = np.where(sign == 0, cosine, -sign * sine) * same
    lanes = np.stack([forward, backward]).astype(jnp.bfloat16)
    return (
        both(coarse, column, 512),
        both(fine, column, 512),
        both(coarse, phase[None, :], 2048),
        both(fine, phase[None, :], 2048),
        lanes,
    )


def tables_kernel(coarse_ref, fine_ref, outer_ref, inner_ref, high_ref, low_ref, twiddle_ref):
    lane = lax.broadcasted_iota(jnp.int32, (32, 128), 1)
    for place in range(16):
        rows = slice(32 * place, 32 * place + 32)
        cosine, sine = coarse_ref[0, place : place + 1], coarse_ref[1, place : place + 1]
        high, low = halves(cosine * fine_ref[0] - sine * fine_ref[1])
        high_ref[rows, :512], low_ref[rows, :512] = high, low
        high, low = halves(sine * fine_ref[0] + cosine * fine_ref[1])
        high_ref[rows, 512:], low_ref[rows, 512:] = high, low
        cosine, sine = outer_ref[0, place : place + 1], outer_ref[1, place : place + 1]
        twiddle_ref[0, rows] = cosine * inner_ref[0] - sine * inner_ref[1]
        turn = sine * inner_ref[0] + cosine * inner_ref[1]
        twiddle_ref[1, rows] = jnp.where(lane < 64, turn, -turn)


def tables(awaited):
    *small, lanes = small_tables()
    waves = jax.ShapeDtypeStruct((512, 1024), bf16)
    shapes = [waves, waves, jax.ShapeDtypeStruct((2, 512, 128), f32)]
    return (*call(tables_kernel, shapes, 8, (), True)(*small, awaited), lanes)


def turned(value):
    lane = lax.broadcasted_iota(jnp.int32, value.shape, 1)
    rolled = pltpu.roll(value, 64, 1)
    return jnp.where(lane < 64, rolled, -rolled)


def rows_transform(value, other, high_ref, low_ref):
    high, low = halves(jnp.concatenate([value, other], axis=0))
    both = dot(high_ref[...], jnp.concatenate([high, low], axis=1))
    return both[:, :128] + both[:, 128:] + dot(low_ref[...], high)


def lanes_transform(value, table):
    high, low = halves(value)
    return dot(high, table) + dot(low, table)


def spectrum_of(packed_ref, high_ref, low_ref, twiddle_ref, lanes_ref):
    value = packed_ref[...].reshape(512, 128)
    value = rows_transform(value, turned(value), high_ref, low_ref)
    value = value * twiddle_ref[0] + pltpu.roll(value, 64, 1) * twiddle_ref[1]
    return lanes_transform(value, lanes_ref[0])


def screened_kernel(packed_ref, high_ref, low_ref, twiddle_ref, lanes_ref, out_ref):
    value = spectrum_of(packed_ref, high_ref, low_ref, twiddle_ref, lanes_ref) * (2048.0**-1.5)
    rolled = pltpu.roll(value, 64, 1)
    first = lax.broadcasted_iota(jnp.int32, value.shape, 1) < 64
    out_ref[0] = jnp.where(first, value, rolled)
    out_ref[1] = jnp.where(first, -rolled, value)


def convolve_kernel(packed_ref, screened_ref, high_ref, low_ref, twiddle_ref, lanes_ref, out_ref):
    value = spectrum_of(packed_ref, high_ref, low_ref, twiddle_ref, lanes_ref)
    value = value * screened_ref[0] + pltpu.roll(value, 64, 1) * screened_ref[1]
    value = lanes_transform(value, lanes_ref[1])
    value = value * twiddle_ref[0] - pltpu.roll(value, 64, 1) * twiddle_ref[1]
    value = rows_transform(value, -turned(value), high_ref, low_ref)
    out_ref[...] = value.reshape(64, 8, 128)


def screened_spectrum(packed, constants):
    shape = jax.ShapeDtypeStruct((2, 512, 128), f32)
    return call(screened_kernel, shape, 8)(packed, *constants)


def convolve(packed, screened, constants):
    shape = jax.ShapeDtypeStruct((64, 8, 128), f32)
    return call(convolve_kernel, shape, 8)(packed, screened, *constants)


def exchange(packed):
    return lax.all_to_all(packed, "energy", split_axis=0, concat_axis=0, tiled=True)


def body(chain_map, chain_source, local_map, local_source, interaction, element_pairs):
    place = lax.axis_index("space").astype(jnp.int32).reshape(1)
    rows = 2 * chain_source.shape[1]
    source = chain_source.reshape(rows, chain_source.shape[2])

    def move(value, *pairs):
        return lax.ppermute(value, "space", pairs)

    arrived = move(source, (0, 1))
    upward = [(leader - 1, leader) for leader in LEADERS]
    downward = [(leader + 1, leader) for leader in LEADERS]
    before = (move(chain_map, *upward), move(source, *upward))
    after = (move(chain_map, *downward), move(source, *downward))
    own = (*split_map(chain_map), source)
    entering, middle, state = on_plane(first_kernel, 1, place, (arrived, *own), (), (source,) * 3)
    for number in range(2, SINGLES + 1):
        arrived = move(state, (number - 1, number))
        entering, state = on_plane(
            single_kernel, number, place, (arrived, *own), (entering, state)
        )
    screened = exchange(pack_array(jnp.swapaxes(interaction, 1, 2)))
    constants = tables(screened)
    screened = screened_spectrum(screened, constants)
    before = (*split_map(before[0], screened), before[1])
    after = (*split_map(after[0], screened), after[1])
    last = SINGLES
    for leader in LEADERS:
        arrived = move(state, (last, leader))
        operands = (arrived, *before, *own, *after)
        entering, middle, state = on_plane(
            triple_kernel, leader, place, operands, (entering, middle, state)
        )
        last = leader
    arrived = move(state, (SINGLES, SINGLES + 1), *((leader, leader + 2) for leader in LEADERS))
    other = move(middle, *((leader, leader + 1) for leader in LEADERS))
    local_high, local_low = split_map(local_map)
    chosen = choose(element_pairs, local_map.shape[2])
    constant = jnp.swapaxes(local_source, 1, 2)
    packed = packed_lesser(arrived, other, entering, local_high, local_low, constant, chosen)
    result = convolve(exchange(packed), screened, constants)
    return jnp.swapaxes(unpack_array(exchange(result)), 1, 2)


def solution(mesh):
    in_specs = (
        P(None, "space", None),
        P(None, "energy", "space"),
        P(None, "space", None),
        P(None, "space", "energy"),
        P(None, "space", "energy"),
        P(None, "space"),
    )
    out_specs = P(None, "space", "energy")

    return jax.shard_map(body, mesh=mesh, in_specs=in_specs, out_specs=out_specs, check_vma=False)
```

```python
import functools

import jax
import jax.numpy as jnp
import numpy as np
from jax import lax
from jax.experimental import pallas as pl
from jax.experimental.pallas import tpu as pltpu
from jax.sharding import PartitionSpec as P


SINGLES = 5
LEADERS = (7, 10, 13)

f32 = jnp.float32
bf16 = jnp.bfloat16


def call(kernel, out_shape, megabytes, scratch=(), awaits=False):
    if awaits:
        vmem = pl.BlockSpec(memory_space=pltpu.VMEM)

        def after(*operands):
            count = len(operands) - 1
            specs = [vmem] * count + [pl.BlockSpec(memory_space=pl.ANY)]

            def body(*refs):
                kernel(*refs[:count], *refs[count + 1 :])

            return pl.pallas_call(
                body,
                out_shape=out_shape,
                in_specs=specs,
                scratch_shapes=list(scratch),
                compiler_params=pltpu.CompilerParams(vmem_limit_bytes=megabytes << 20),
            )(*operands)

        return after
    return pl.pallas_call(
        kernel,
        out_shape=out_shape,
        scratch_shapes=list(scratch),
        compiler_params=pltpu.CompilerParams(vmem_limit_bytes=megabytes << 20),
    )


def halves(value):
    high = value.astype(bf16)
    return high, (value - high.astype(f32)).astype(bf16)


def dot(left, right):
    return jnp.dot(left, right, preferred_element_type=f32)


def complex_rows_dot(rows, high_ref, low_ref):
    count = rows.shape[0]
    high, low = halves(rows)
    both = dot(jnp.concatenate([high, low], axis=0), high_ref[...])
    product = both[:count] + both[count:] + dot(high, low_ref[...])
    half, width = count // 2, product.shape[1] // 2
    real = product[:half, :width] - product[half:, width:]
    imag = product[:half, width:] + product[half:, :width]
    return real, imag


def split_kernel(map_ref, high_ref, low_ref):
    width = map_ref.shape[2]
    for part in range(2):
        high, low = halves(map_ref[part])
        high_ref[:, part * width : (part + 1) * width] = high
        low_ref[:, part * width : (part + 1) * width] = low


def split_map(value, *awaited):
    shape = jax.ShapeDtypeStruct((value.shape[1], 2 * value.shape[2]), bf16)
    return call(split_kernel, [shape, shape], 8, (), bool(awaited))(value, *awaited)


def advanced(state, high_ref, low_ref, source_ref):
    real, imag = complex_rows_dot(state, high_ref, low_ref)
    return jnp.concatenate([real, imag], axis=0) + source_ref[...]


def first_kernel(number, place_ref, arrived_ref, *refs):
    operands, (entering_ref, middle_ref, state_ref) = refs[:3], refs[3:]
    middle_ref[...] = jnp.zeros_like(middle_ref)

    @pl.when(place_ref[0] == number)
    def _():
        arrived = arrived_ref[...]
        entering_ref[...] = arrived
        state_ref[...] = advanced(arrived, *operands)

    @pl.when(place_ref[0] != number)
    def _():
        entering_ref[...] = jnp.zeros_like(entering_ref)
        state_ref[...] = jnp.zeros_like(state_ref)


def single_kernel(number, place_ref, arrived_ref, *refs):
    operands, held, (entering_ref, state_ref) = refs[:3], refs[3:5], refs[5:]

    @pl.when(place_ref[0] == number)
    def _():
        arrived = arrived_ref[...]
        entering_ref[...] = arrived
        state_ref[...] = advanced(arrived, *operands)

    @pl.when(place_ref[0] != number)
    def _():
        for before_ref, after_ref in zip(held, (entering_ref, state_ref)):
            after_ref[...] = before_ref[...]


def triple_kernel(number, place_ref, arrived_ref, *refs):
    before, own, after = refs[0:3], refs[3:6], refs[6:9]
    held, (entering_ref, middle_ref, state_ref) = refs[9:12], refs[12:]

    @pl.when(place_ref[0] == number)
    def _():
        first = advanced(arrived_ref[...], *before)
        entering_ref[...] = first
        second = advanced(first, *own)
        middle_ref[...] = second
        state_ref[...] = advanced(second, *after)

    @pl.when(place_ref[0] != number)
    def _():
        for before_ref, after_ref in zip(held, (entering_ref, middle_ref, state_ref)):
            after_ref[...] = before_ref[...]


def on_plane(kernel, number, place, operands, held, fresh=()):
    vmem = pl.BlockSpec(memory_space=pltpu.VMEM)
    results = (*held, *fresh)
    return pl.pallas_call(
        functools.partial(kernel, number),
        out_shape=[jax.ShapeDtypeStruct(value.shape, value.dtype) for value in results],
        in_specs=[pl.BlockSpec(memory_space=pltpu.SMEM)] + [vmem] * (len(operands) + len(held)),
        out_specs=[vmem] * len(results),
        compiler_params=pltpu.CompilerParams(vmem_limit_bytes=6 << 20),
    )(place, *operands, *held)


def swap_blocks(parts):
    block = lax.broadcasted_iota(jnp.int32, parts[0].shape, 1) // 16
    for step in (1, 2, 4):
        clear = (block & step) == 0
        swapped = list(parts)
        for place in range(8):
            if place & step == 0:
                lower, upper = parts[place], parts[place + step]
                swapped[place] = jnp.where(clear, lower, pltpu.roll(upper, 16 * step, 1))
                swapped[place + step] = jnp.where(clear, pltpu.roll(lower, 128 - 16 * step, 1), upper)
        parts = swapped
    return parts


def pack(stage_ref, packed_ref):
    for group in range(8):
        parts = [stage_ref[b // 4, group, pl.ds(b % 4, 8, stride=4), :] for b in range(8)]
        for place, tile in enumerate(swap_blocks(parts)):
            packed_ref[8 * group + place] = tile


def pack_kernel(values_ref, packed_ref, stage_ref):
    for part in range(2):
        for group in range(8):
            stage_ref[part, group] = values_ref[part, :, group * 128 : (group + 1) * 128]
    pack(stage_ref, packed_ref)


def unpack_kernel(packed_ref, values_ref, stage_ref):
    for group in range(8):
        parts = [packed_ref[8 * group + place] for place in range(8)]
        for b, tile in enumerate(swap_blocks(parts)):
            stage_ref[b // 4, group, pl.ds(b % 4, 8, stride=4), :] = tile
    for part in range(2):
        for group in range(8):
            values_ref[part, :, group * 128 : (group + 1) * 128] = stage_ref[part, group]


def pack_array(values, awaited):
    shape = jax.ShapeDtypeStruct((64, 8, 128), f32)
    scratch = [pltpu.VMEM((2, 8, 32, 128), f32)]
    return call(pack_kernel, shape, 4, scratch, True)(values, awaited)


def unpack_array(packed):
    shape = jax.ShapeDtypeStruct((2, 32, 1024), f32)
    return call(unpack_kernel, shape, 4, [pltpu.VMEM((2, 8, 32, 128), f32)])(packed)


def choose_kernel(pairs_ref, chosen_ref):
    orbitals, count = chosen_ref.shape[0], pairs_ref.shape[1]
    for side in range(2):
        for group in range(count // 128):
            wanted = pairs_ref[side : side + 1, group * 128 : (group + 1) * 128]
            rows = lax.broadcasted_iota(jnp.int32, (orbitals, 128), 0)
            column = side * count + group * 128
            chosen_ref[:, column : column + 128] = jnp.where(rows == wanted, 1.0, 0.0).astype(bf16)


def choose(pairs, orbitals):
    shape = jax.ShapeDtypeStruct((orbitals, 2 * pairs.shape[1]), bf16)
    return call(choose_kernel, shape, 8)(pairs)


def lesser_kernel(
    arrived_ref, other_ref, entering_ref, high_ref, low_ref, source_ref, chosen_ref, packed_ref, stage_ref
):
    state = entering_ref[...] + (arrived_ref[...] + other_ref[...])
    real, imag = complex_rows_dot(state, high_ref, low_ref)
    wave = jnp.concatenate([real + source_ref[0], imag + source_ref[1]], axis=0)
    rows, half = wave.shape[0], wave.shape[0] // 2
    high, low = halves(wave)
    both = dot(jnp.concatenate([high, low], axis=0), chosen_ref[...])
    taken = both[:rows] + both[rows:]
    count = taken.shape[1] // 2
    left_re, left_im = taken[:half, :count], taken[half:, :count]
    right_re, right_im = taken[:half, count:], taken[half:, count:]
    lesser_re = left_re * right_re + left_im * right_im
    lesser_im = left_im * right_re - left_re * right_im
    for group in range(8):
        stage_ref[0, group] = lesser_re[:, group * 128 : (group + 1) * 128]
        stage_ref[1, group] = lesser_im[:, group * 128 : (group + 1) * 128]
    pack(stage_ref, packed_ref)


def packed_lesser(arrived, other, entering, high, low, source, chosen):
    shape = jax.ShapeDtypeStruct((64, 8, 128), f32)
    scratch = [pltpu.VMEM((2, 8, 32, 128), f32)]
    return call(lesser_kernel, shape, 14, scratch)(
        arrived, other, entering, high, low, source, chosen
    )


def small_tables():
    coarse, fine = 32 * np.arange(16)[:, None], np.arange(32)[:, None]
    column, lane = np.arange(512)[None, :], np.arange(128)
    imaginary, phase, element = lane // 64, lane // 16 % 4, lane % 16

    def both(rows, columns, period):
        angle = 2.0 * np.pi / period * (rows * columns % period)
        return np.stack([np.cos(angle), np.sin(angle)]).astype(np.float32)

    turns = phase[:, None] * phase[None, :] % 4
    cosine, sine = np.array([1, 0, -1, 0])[turns], np.array([0, 1, 0, -1])[turns]
    sign = imaginary[:, None] - imaginary[None, :]
    same = element[:, None] == element[None, :]
    forward = np.where(sign == 0, cosine, sign * sine) * same
    backward = np.where(sign == 0, cosine, -sign * sine) * same
    lanes = np.stack([forward, backward]).astype(jnp.bfloat16)
    return (
        both(coarse, column, 512),
        both(fine, column, 512),
        both(coarse, phase[None, :], 2048),
        both(fine, phase[None, :], 2048),
        lanes,
    )


def tables_kernel(coarse_ref, fine_ref, outer_ref, inner_ref, high_ref, low_ref, twiddle_ref):
    lane = lax.broadcasted_iota(jnp.int32, (32, 128), 1)
    for place in range(16):
        rows = slice(32 * place, 32 * place + 32)
        cosine, sine = coarse_ref[0, place : place + 1], coarse_ref[1, place : place + 1]
        high, low = halves(cosine * fine_ref[0] - sine * fine_ref[1])
        high_ref[rows, :512], low_ref[rows, :512] = high, low
        high, low = halves(sine * fine_ref[0] + cosine * fine_ref[1])
        high_ref[rows, 512:], low_ref[rows, 512:] = high, low
        cosine, sine = outer_ref[0, place : place + 1], outer_ref[1, place : place + 1]
        twiddle_ref[0, rows] = cosine * inner_ref[0] - sine * inner_ref[1]
        turn = sine * inner_ref[0] + cosine * inner_ref[1]
        twiddle_ref[1, rows] = jnp.where(lane < 64, turn, -turn)


def tables(awaited):
    *small, lanes = small_tables()
    waves = jax.ShapeDtypeStruct((512, 1024), bf16)
    shapes = [waves, waves, jax.ShapeDtypeStruct((2, 512, 128), f32)]
    return (*call(tables_kernel, shapes, 8, (), True)(*small, awaited), lanes)


def turned(value):
    lane = lax.broadcasted_iota(jnp.int32, value.shape, 1)
    rolled = pltpu.roll(value, 64, 1)
    return jnp.where(lane < 64, rolled, -rolled)


def rows_transform(value, other, high_ref, low_ref):
    high, low = halves(jnp.concatenate([value, other], axis=0))
    both = dot(high_ref[...], jnp.concatenate([high, low], axis=1))
    return both[:, :128] + both[:, 128:] + dot(low_ref[...], high)


def lanes_transform(value, table):
    high, low = halves(value)
    return dot(high, table) + dot(low, table)


def spectrum_of(packed_ref, high_ref, low_ref, twiddle_ref, lanes_ref):
    value = packed_ref[...].reshape(512, 128)
    value = rows_transform(value, turned(value), high_ref, low_ref)
    value = value * twiddle_ref[0] + pltpu.roll(value, 64, 1) * twiddle_ref[1]
    return lanes_transform(value, lanes_ref[0])


def screened_kernel(packed_ref, high_ref, low_ref, twiddle_ref, lanes_ref, out_ref):
    value = spectrum_of(packed_ref, high_ref, low_ref, twiddle_ref, lanes_ref) * (2048.0**-1.5)
    rolled = pltpu.roll(value, 64, 1)
    first = lax.broadcasted_iota(jnp.int32, value.shape, 1) < 64
    out_ref[0] = jnp.where(first, value, rolled)
    out_ref[1] = jnp.where(first, -rolled, value)


def convolve_kernel(packed_ref, screened_ref, high_ref, low_ref, twiddle_ref, lanes_ref, out_ref):
    value = spectrum_of(packed_ref, high_ref, low_ref, twiddle_ref, lanes_ref)
    value = value * screened_ref[0] + pltpu.roll(value, 64, 1) * screened_ref[1]
    value = lanes_transform(value, lanes_ref[1])
    value = value * twiddle_ref[0] - pltpu.roll(value, 64, 1) * twiddle_ref[1]
    value = rows_transform(value, -turned(value), high_ref, low_ref)
    out_ref[...] = value.reshape(64, 8, 128)


def screened_spectrum(packed, constants):
    shape = jax.ShapeDtypeStruct((2, 512, 128), f32)
    return call(screened_kernel, shape, 8)(packed, *constants)


def convolve(packed, screened, constants):
    shape = jax.ShapeDtypeStruct((64, 8, 128), f32)
    return call(convolve_kernel, shape, 8)(packed, screened, *constants)


def exchange(packed):
    return lax.all_to_all(packed, "energy", split_axis=0, concat_axis=0, tiled=True)


def body(chain_map, chain_source, local_map, local_source, interaction, element_pairs):
    place = lax.axis_index("space").astype(jnp.int32).reshape(1)
    rows = 2 * chain_source.shape[1]
    source = chain_source.reshape(rows, chain_source.shape[2])

    def move(value, *pairs):
        return lax.ppermute(value, "space", pairs)

    arrived = move(source, (0, 1))
    upward = [(leader - 1, leader) for leader in LEADERS]
    downward = [(leader + 1, leader) for leader in LEADERS]
    maps = []
    for order, chosen in enumerate((slice(0, 1), slice(1, None))):
        maps.append([move(chain_map, *pairs[chosen]) for pairs in (upward, downward)])
        if order == 0:
            source_before, source_after = move(source, *upward), move(source, *downward)
    own = (*split_map(chain_map), source)
    entering, middle, state = on_plane(first_kernel, 1, place, (arrived, *own), (), (source,) * 3)
    for number in range(2, SINGLES + 1):
        arrived = move(state, (number - 1, number))
        if number == SINGLES - 1:
            screened = pack_array(jnp.swapaxes(interaction, 1, 2), entering)
            screened = exchange(screened)
        entering, state = on_plane(
            single_kernel, number, place, (arrived, *own), (entering, state)
        )
    last, awaited = SINGLES, ()
    for order, leader in enumerate(LEADERS):
        arrived = move(state, (last, leader))
        if order < 2:
            before, after = (split_map(value, *awaited) for value in maps[order])
        operands = (arrived, *before, source_before, *own, *after, source_after)
        entering, middle, state = on_plane(
            triple_kernel, leader, place, operands, (entering, middle, state)
        )
        if order == 0:
            constants = tables(entering)
            screened = screened_spectrum(screened, constants)
            awaited = (screened,)
        last = leader
    arrived = move(state, (SINGLES, SINGLES + 1), *((leader, leader + 2) for leader in LEADERS))
    other = move(middle, *((leader, leader + 1) for leader in LEADERS))
    local_high, local_low = split_map(local_map)
    chosen = choose(element_pairs, local_map.shape[2])
    constant = jnp.swapaxes(local_source, 1, 2)
    packed = packed_lesser(arrived, other, entering, local_high, local_low, constant, chosen)
    result = convolve(exchange(packed), screened, constants)
    return jnp.swapaxes(unpack_array(exchange(result)), 1, 2)


def solution(mesh):
    in_specs = (
        P(None, "space", None),
        P(None, "energy", "space"),
        P(None, "space", None),
        P(None, "space", "energy"),
        P(None, "space", "energy"),
        P(None, "space"),
    )
    out_specs = P(None, "space", "energy")

    return jax.shard_map(body, mesh=mesh, in_specs=in_specs, out_specs=out_specs, check_vma=False)
```

```python
import functools

import jax
import jax.numpy as jnp
import numpy as np
from jax import lax
from jax.experimental import pallas as pl
from jax.experimental.pallas import tpu as pltpu
from jax.sharding import PartitionSpec as P


SINGLES = 5
LEADERS = (7, 10, 13)

f32 = jnp.float32
bf16 = jnp.bfloat16


def call(kernel, out_shape, megabytes, scratch=(), awaits=0):
    if awaits:
        vmem = pl.BlockSpec(memory_space=pltpu.VMEM)

        def after(*operands):
            count = len(operands) - awaits
            specs = [vmem] * count + [pl.BlockSpec(memory_space=pl.ANY)] * awaits

            def body(*refs):
                kernel(*refs[:count], *refs[count + awaits :])

            return pl.pallas_call(
                body,
                out_shape=out_shape,
                in_specs=specs,
                scratch_shapes=list(scratch),
                compiler_params=pltpu.CompilerParams(vmem_limit_bytes=megabytes << 20),
            )(*operands)

        return after
    return pl.pallas_call(
        kernel,
        out_shape=out_shape,
        scratch_shapes=list(scratch),
        compiler_params=pltpu.CompilerParams(vmem_limit_bytes=megabytes << 20),
    )


def halves(value):
    high = value.astype(bf16)
    return high, (value - high.astype(f32)).astype(bf16)


def dot(left, right):
    return jnp.dot(left, right, preferred_element_type=f32)


def complex_rows_dot(rows, high_ref, low_ref):
    count = rows.shape[0]
    high, low = halves(rows)
    both = dot(jnp.concatenate([high, low], axis=0), high_ref[...])
    product = both[:count] + both[count:] + dot(high, low_ref[...])
    half, width = count // 2, product.shape[1] // 2
    real = product[:half, :width] - product[half:, width:]
    imag = product[:half, width:] + product[half:, :width]
    return real, imag


def split_kernel(map_ref, high_ref, low_ref):
    width = map_ref.shape[2]
    for part in range(2):
        high, low = halves(map_ref[part])
        high_ref[:, part * width : (part + 1) * width] = high
        low_ref[:, part * width : (part + 1) * width] = low


def split_map(value, *awaited):
    shape = jax.ShapeDtypeStruct((value.shape[1], 2 * value.shape[2]), bf16)
    return call(split_kernel, [shape, shape], 8, (), len(awaited))(value, *awaited)


def split_both_kernel(first_ref, second_ref, *out_refs):
    split_kernel(first_ref, *out_refs[:2])
    split_kernel(second_ref, *out_refs[2:])


def split_both(first, second, *awaited):
    shape = jax.ShapeDtypeStruct((first.shape[1], 2 * first.shape[2]), bf16)
    split = call(split_both_kernel, [shape] * 4, 10, (), len(awaited))
    return split(first, second, *awaited)


def advanced(state, high_ref, low_ref, source_ref):
    real, imag = complex_rows_dot(state, high_ref, low_ref)
    return jnp.concatenate([real, imag], axis=0) + source_ref[...]


def first_kernel(number, place_ref, arrived_ref, *refs):
    operands, (entering_ref, middle_ref, state_ref) = refs[:3], refs[3:]
    middle_ref[...] = jnp.zeros_like(middle_ref)

    @pl.when(place_ref[0] == number)
    def _():
        arrived = arrived_ref[...]
        entering_ref[...] = arrived
        state_ref[...] = advanced(arrived, *operands)

    @pl.when(place_ref[0] != number)
    def _():
        entering_ref[...] = jnp.zeros_like(entering_ref)
        state_ref[...] = jnp.zeros_like(state_ref)


def single_kernel(number, place_ref, arrived_ref, *refs):
    operands, held, (entering_ref, state_ref) = refs[:3], refs[3:5], refs[5:]

    @pl.when(place_ref[0] == number)
    def _():
        arrived = arrived_ref[...]
        entering_ref[...] = arrived
        state_ref[...] = advanced(arrived, *operands)

    @pl.when(place_ref[0] != number)
    def _():
        for before_ref, after_ref in zip(held, (entering_ref, state_ref)):
            after_ref[...] = before_ref[...]


def triple_kernel(number, place_ref, arrived_ref, *refs):
    before, own, after = refs[0:3], refs[3:6], refs[6:9]
    held, (entering_ref, middle_ref, state_ref) = refs[9:12], refs[12:]

    @pl.when(place_ref[0] == number)
    def _():
        first = advanced(arrived_ref[...], *before)
        entering_ref[...] = first
        second = advanced(first, *own)
        middle_ref[...] = second
        state_ref[...] = advanced(second, *after)

    @pl.when(place_ref[0] != number)
    def _():
        for before_ref, after_ref in zip(held, (entering_ref, middle_ref, state_ref)):
            after_ref[...] = before_ref[...]


def on_plane(kernel, number, place, operands, held, fresh=()):
    vmem = pl.BlockSpec(memory_space=pltpu.VMEM)
    results = (*held, *fresh)
    return pl.pallas_call(
        functools.partial(kernel, number),
        out_shape=[jax.ShapeDtypeStruct(value.shape, value.dtype) for value in results],
        in_specs=[pl.BlockSpec(memory_space=pltpu.SMEM)] + [vmem] * (len(operands) + len(held)),
        out_specs=[vmem] * len(results),
        compiler_params=pltpu.CompilerParams(vmem_limit_bytes=6 << 20),
    )(place, *operands, *held)


def swap_blocks(parts):
    block = lax.broadcasted_iota(jnp.int32, parts[0].shape, 1) // 16
    for step in (1, 2, 4):
        clear = (block & step) == 0
        swapped = list(parts)
        for place in range(8):
            if place & step == 0:
                lower, upper = parts[place], parts[place + step]
                swapped[place] = jnp.where(clear, lower, pltpu.roll(upper, 16 * step, 1))
                swapped[place + step] = jnp.where(clear, pltpu.roll(lower, 128 - 16 * step, 1), upper)
        parts = swapped
    return parts


def pack(stage_ref, packed_ref):
    for group in range(8):
        parts = [stage_ref[b // 4, group, pl.ds(b % 4, 8, stride=4), :] for b in range(8)]
        for place, tile in enumerate(swap_blocks(parts)):
            packed_ref[8 * group + place] = tile


def pack_kernel(values_ref, packed_ref, stage_ref):
    for part in range(2):
        for group in range(8):
            stage_ref[part, group] = values_ref[part, :, group * 128 : (group + 1) * 128]
    pack(stage_ref, packed_ref)


def unpack_kernel(packed_ref, values_ref, stage_ref):
    for group in range(8):
        parts = [packed_ref[8 * group + place] for place in range(8)]
        for b, tile in enumerate(swap_blocks(parts)):
            stage_ref[b // 4, group, pl.ds(b % 4, 8, stride=4), :] = tile
    for part in range(2):
        for group in range(8):
            values_ref[part, :, group * 128 : (group + 1) * 128] = stage_ref[part, group]


def pack_array(values, awaited):
    shape = jax.ShapeDtypeStruct((64, 8, 128), f32)
    scratch = [pltpu.VMEM((2, 8, 32, 128), f32)]
    return call(pack_kernel, shape, 4, scratch, 1)(values, awaited)


def unpack_array(packed):
    shape = jax.ShapeDtypeStruct((2, 32, 1024), f32)
    return call(unpack_kernel, shape, 4, [pltpu.VMEM((2, 8, 32, 128), f32)])(packed)


def choose_kernel(pairs_ref, chosen_ref):
    orbitals, count = chosen_ref.shape[0], pairs_ref.shape[1]
    for side in range(2):
        for group in range(count // 128):
            wanted = pairs_ref[side : side + 1, group * 128 : (group + 1) * 128]
            rows = lax.broadcasted_iota(jnp.int32, (orbitals, 128), 0)
            column = side * count + group * 128
            chosen_ref[:, column : column + 128] = jnp.where(rows == wanted, 1.0, 0.0).astype(bf16)


def choose(pairs, orbitals, *awaited):
    shape = jax.ShapeDtypeStruct((orbitals, 2 * pairs.shape[1]), bf16)
    return call(choose_kernel, shape, 8, (), len(awaited))(pairs, *awaited)


def lesser_kernel(
    arrived_ref, other_ref, entering_ref, high_ref, low_ref, source_ref, chosen_ref, packed_ref, stage_ref
):
    state = entering_ref[...] + (arrived_ref[...] + other_ref[...])
    real, imag = complex_rows_dot(state, high_ref, low_ref)
    wave = jnp.concatenate([real + source_ref[0], imag + source_ref[1]], axis=0)
    rows, half = wave.shape[0], wave.shape[0] // 2
    high, low = halves(wave)
    both = dot(jnp.concatenate([high, low], axis=0), chosen_ref[...])
    taken = both[:rows] + both[rows:]
    count = taken.shape[1] // 2
    left_re, left_im = taken[:half, :count], taken[half:, :count]
    right_re, right_im = taken[:half, count:], taken[half:, count:]
    lesser_re = left_re * right_re + left_im * right_im
    lesser_im = left_im * right_re - left_re * right_im
    for group in range(8):
        stage_ref[0, group] = lesser_re[:, group * 128 : (group + 1) * 128]
        stage_ref[1, group] = lesser_im[:, group * 128 : (group + 1) * 128]
    pack(stage_ref, packed_ref)


def packed_lesser(arrived, other, entering, high, low, source, chosen):
    shape = jax.ShapeDtypeStruct((64, 8, 128), f32)
    scratch = [pltpu.VMEM((2, 8, 32, 128), f32)]
    return call(lesser_kernel, shape, 14, scratch)(
        arrived, other, entering, high, low, source, chosen
    )


def small_tables():
    coarse, fine = 32 * np.arange(16)[:, None], np.arange(32)[:, None]
    column, lane = np.arange(512)[None, :], np.arange(128)
    imaginary, phase, element = lane // 64, lane // 16 % 4, lane % 16

    def both(rows, columns, period):
        angle = 2.0 * np.pi / period * (rows * columns % period)
        return np.stack([np.cos(angle), np.sin(angle)]).astype(np.float32)

    turns = phase[:, None] * phase[None, :] % 4
    cosine, sine = np.array([1, 0, -1, 0])[turns], np.array([0, 1, 0, -1])[turns]
    sign = imaginary[:, None] - imaginary[None, :]
    same = element[:, None] == element[None, :]
    forward = np.where(sign == 0, cosine, sign * sine) * same
    backward = np.where(sign == 0, cosine, -sign * sine) * same
    lanes = np.stack([forward, backward]).astype(jnp.bfloat16)
    return (
        both(coarse, column, 512),
        both(fine, column, 512),
        both(coarse, phase[None, :], 2048),
        both(fine, phase[None, :], 2048),
        lanes,
    )


def tables_kernel(coarse_ref, fine_ref, outer_ref, inner_ref, high_ref, low_ref, twiddle_ref):
    lane = lax.broadcasted_iota(jnp.int32, (32, 128), 1)
    for place in range(16):
        rows = slice(32 * place, 32 * place + 32)
        cosine, sine = coarse_ref[0, place : place + 1], coarse_ref[1, place : place + 1]
        high, low = halves(cosine * fine_ref[0] - sine * fine_ref[1])
        high_ref[rows, :512], low_ref[rows, :512] = high, low
        high, low = halves(sine * fine_ref[0] + cosine * fine_ref[1])
        high_ref[rows, 512:], low_ref[rows, 512:] = high, low
        cosine, sine = outer_ref[0, place : place + 1], outer_ref[1, place : place + 1]
        twiddle_ref[0, rows] = cosine * inner_ref[0] - sine * inner_ref[1]
        turn = sine * inner_ref[0] + cosine * inner_ref[1]
        twiddle_ref[1, rows] = jnp.where(lane < 64, turn, -turn)


def tables(*awaited):
    *small, lanes = small_tables()
    waves = jax.ShapeDtypeStruct((512, 1024), bf16)
    shapes = [waves, waves, jax.ShapeDtypeStruct((2, 512, 128), f32)]
    return (*call(tables_kernel, shapes, 8, (), len(awaited))(*small, *awaited), lanes)


def turned(value):
    lane = lax.broadcasted_iota(jnp.int32, value.shape, 1)
    rolled = pltpu.roll(value, 64, 1)
    return jnp.where(lane < 64, rolled, -rolled)


def rows_transform(value, other, high_ref, low_ref):
    high, low = halves(jnp.concatenate([value, other], axis=0))
    both = dot(high_ref[...], jnp.concatenate([high, low], axis=1))
    return both[:, :128] + both[:, 128:] + dot(low_ref[...], high)


def lanes_transform(value, table):
    high, low = halves(value)
    return dot(high, table) + dot(low, table)


def spectrum_of(packed_ref, high_ref, low_ref, twiddle_ref, lanes_ref):
    value = packed_ref[...].reshape(512, 128)
    value = rows_transform(value, turned(value), high_ref, low_ref)
    value = value * twiddle_ref[0] + pltpu.roll(value, 64, 1) * twiddle_ref[1]
    return lanes_transform(value, lanes_ref[0])


def screened_kernel(packed_ref, high_ref, low_ref, twiddle_ref, lanes_ref, out_ref):
    value = spectrum_of(packed_ref, high_ref, low_ref, twiddle_ref, lanes_ref) * (2048.0**-1.5)
    rolled = pltpu.roll(value, 64, 1)
    first = lax.broadcasted_iota(jnp.int32, value.shape, 1) < 64
    out_ref[0] = jnp.where(first, value, rolled)
    out_ref[1] = jnp.where(first, -rolled, value)


def convolve_kernel(packed_ref, screened_ref, high_ref, low_ref, twiddle_ref, lanes_ref, out_ref):
    value = spectrum_of(packed_ref, high_ref, low_ref, twiddle_ref, lanes_ref)
    value = value * screened_ref[0] + pltpu.roll(value, 64, 1) * screened_ref[1]
    value = lanes_transform(value, lanes_ref[1])
    value = value * twiddle_ref[0] - pltpu.roll(value, 64, 1) * twiddle_ref[1]
    value = rows_transform(value, -turned(value), high_ref, low_ref)
    out_ref[...] = value.reshape(64, 8, 128)


def screened_spectrum(packed, constants):
    shape = jax.ShapeDtypeStruct((2, 512, 128), f32)
    return call(screened_kernel, shape, 8)(packed, *constants)


def convolve(packed, screened, constants):
    shape = jax.ShapeDtypeStruct((64, 8, 128), f32)
    return call(convolve_kernel, shape, 8)(packed, screened, *constants)


def exchange(packed):
    return lax.all_to_all(packed, "energy", split_axis=0, concat_axis=0, tiled=True)


def body(chain_map, chain_source, local_map, local_source, interaction, element_pairs):
    place = lax.axis_index("space").astype(jnp.int32).reshape(1)
    rows = 2 * chain_source.shape[1]
    source = chain_source.reshape(rows, chain_source.shape[2])

    def move(value, *pairs):
        return lax.ppermute(value, "space", pairs)

    arrived = move(source, (0, 1))
    upward = [(leader - 1, leader) for leader in LEADERS]
    downward = [(leader + 1, leader) for leader in LEADERS]
    maps = []
    for order, chosen in enumerate((slice(0, 1), slice(1, None))):
        maps.append([move(chain_map, *pairs[chosen]) for pairs in (upward, downward)])
        if order == 0:
            source_before, source_after = move(source, *upward), move(source, *downward)
    own = (*split_map(chain_map), source)
    entering, middle, state = on_plane(first_kernel, 1, place, (arrived, *own), (), (source,) * 3)
    for number in range(2, SINGLES + 1):
        arrived = move(state, (number - 1, number))
        if number == SINGLES - 1:
            screened = pack_array(jnp.swapaxes(interaction, 1, 2), entering)
            screened = exchange(screened)
        entering, state = on_plane(
            single_kernel, number, place, (arrived, *own), (entering, state)
        )
    last, awaited = SINGLES, ()
    for order, leader in enumerate(LEADERS):
        arrived = move(state, (last, leader))
        if order < 2:
            split = split_both(*maps[order], *awaited)
        operands = (arrived, *split[:2], source_before, *own, *split[2:], source_after)
        entering, middle, state = on_plane(
            triple_kernel, leader, place, operands, (entering, middle, state)
        )
        last, awaited = leader, (entering,)
    other = move(middle, *((leader, leader + 1) for leader in LEADERS))
    arrived = move(state, (SINGLES, SINGLES + 1), *((leader, leader + 2) for leader in LEADERS))
    constants = tables(screened, entering)
    screened = screened_spectrum(screened, constants)
    chosen = choose(element_pairs, local_map.shape[2], screened)
    local_high, local_low = split_map(local_map, chosen)
    constant = jnp.swapaxes(local_source, 1, 2)
    packed = packed_lesser(arrived, other, entering, local_high, local_low, constant, chosen)
    result = convolve(exchange(packed), screened, constants)
    return jnp.swapaxes(unpack_array(exchange(result)), 1, 2)


def solution(mesh):
    in_specs = (
        P(None, "space", None),
        P(None, "energy", "space"),
        P(None, "space", None),
        P(None, "space", "energy"),
        P(None, "space", "energy"),
        P(None, "space"),
    )
    out_specs = P(None, "space", "energy")

    return jax.shard_map(body, mesh=mesh, in_specs=in_specs, out_specs=out_specs, check_vma=False)
```
